512 devices in a mesh: gx: 32 (over y, x, core), gy: 16 (over z).
Axes of the slice: x: 4, y: 4, z: 16, core: 2. Of those that a mesh axis runs over, the one named last changes fastest.
Arguments:
- basis: bfloat16 [16, 4, 512, 4096], P(None, None, 'gy', 'gx'), may hold values from -56 to 56
- mobility: bfloat16 [4, 512, 4096], P(None, 'gy', 'gx'), may hold values from 0.12 to 8.2
- accumulation: float32 [4, 512, 4096], P(None, 'gy', 'gx'), may hold values from 0.03 to 0.32
- residual: float32 [4, 512, 4096], P(None, 'gy', 'gx'), may hold values from -140 to 140
Outputs:
- correction: float32 [4, 512, 4096], P(None, 'gy', 'gx')
- coarse_solution: float32 [32, 16, 16], P('gx', 'gy')
The draws below stay inside these ranges and needn't reach their ends.
All inputs are finite; a program needn't handle non-finite values.
Results may differ from the reference program's by a relative error of at most 0.0003.
Values may be sent and summed in bfloat16 or wider, within the bound.
A program may use at most 64 MiB of HBM per device.

```python
import jax
import jax.numpy as jnp
from jax import lax

K = 16
CX = 128
CY = 32
CZ = 4
ITERS = 2
SUBX = 32
SUBY = 16
NX = 4096
NY = 512
N_GX = 32
N_GY = 16


def cosine_table(mode_count, length):
    wavenumber = jnp.arange(mode_count, dtype=jnp.float32)
    position = (jnp.arange(length, dtype=jnp.float32) + 0.5) / length
    return jnp.cos(jnp.pi * wavenumber[:, None] * position[None, :])


def mode_weights(count_z, count_y, count_x):
    along_z = jnp.arange(count_z, dtype=jnp.float32)
    along_y = jnp.arange(count_y, dtype=jnp.float32)
    along_x = jnp.arange(count_x, dtype=jnp.float32)
    return 1.0 / (1.0 + along_z[:, None, None] + along_y[None, :, None] + along_x[None, None, :])


def global_smooth(key):
    coefficient = jax.random.truncated_normal(key, -3.0, 3.0, (2, 8, 8)) * mode_weights(2, 8, 8)
    return jnp.einsum('cde,cz,dy,ex->zyx', coefficient, cosine_table(2, CZ), cosine_table(8, NY), cosine_table(8, NX))


def draw_basis(key, part):
    coefficient_key, jitter_key = jax.random.split(jax.random.fold_in(key, 404), 2)
    weight = mode_weights(4, 4, 4)
    coefficient = jax.random.truncated_normal(coefficient_key, -3.0, 3.0, (K, SUBX, SUBY, 4, 4, 4)) * weight
    jitter = 0.1 * jax.random.truncated_normal(jitter_key, -4.0, 4.0, (K, CZ, NY, NX))
    smooth = jnp.einsum('kabcde,cz,dq,ep->kzbqap', coefficient, cosine_table(4, CZ), cosine_table(4, CY), cosine_table(4, CX))
    return (smooth.reshape(K, CZ, NY, NX) + jitter).astype(jnp.bfloat16)


def draw_mobility(key, part):
    smooth_key, jitter_key = jax.random.split(jax.random.fold_in(key, 101))
    smooth = global_smooth(smooth_key)
    jitter = jax.random.uniform(jitter_key, (CZ, NY, NX), minval=-0.6, maxval=0.6)
    return jnp.exp(1.5 * jnp.tanh(0.5 * smooth) + jitter).astype(jnp.bfloat16)


def draw_accumulation(key, part):
    smooth_key, jitter_key = jax.random.split(jax.random.fold_in(key, 202))
    smooth = global_smooth(smooth_key)
    jitter = jax.random.uniform(jitter_key, (CZ, NY, NX), minval=-0.35, maxval=0.35)
    return 0.1 * jnp.exp(0.8 * jnp.tanh(0.5 * smooth) + jitter)


def draw_residual(key, part):
    smooth_key, jitter_key = jax.random.split(jax.random.fold_in(key, 303))
    smooth = global_smooth(smooth_key)
    column = jnp.arange(NX, dtype=jnp.float32) / max(NX - 1, 1)
    slope_factor = jnp.broadcast_to(1.0 + 2.0 * column[None, None, :], (CZ, NY, NX))
    jitter = jax.random.truncated_normal(jitter_key, -4.0, 4.0, (CZ, NY, NX))
    return slope_factor * (0.25 * smooth + 0.15 * jitter)


def setup_inputs(seed: int = 0) -> dict:
    arg_keys = jax.random.split(jax.random.key(seed), 5)
    return {
        "basis": draw_basis(jax.random.fold_in(arg_keys[4], 71), 0),
        "mobility": draw_mobility(jax.random.fold_in(arg_keys[4], 71), 0),
        "accumulation": draw_accumulation(jax.random.fold_in(arg_keys[4], 71), 0),
        "residual": draw_residual(jax.random.fold_in(arg_keys[4], 71), 0),
    }


epsilon = 1e-6
vertical_ratio = 0.1


def harmonic(first, second):
    return 2.0 * first * second / (first + second)


def gram_sum(weighted, other):
    return jnp.einsum('kzyx,lzyx->kl', weighted, other, precision=lax.Precision.HIGHEST)


def face_blocks(padded_basis, padded_mobility, accumulation):
    interior = padded_basis[:, :, 1:-1, 1:-1]
    cell_mobility = padded_mobility[:, 1:-1, 1:-1]
    self_block = gram_sum(interior * accumulation, interior)
    conduct_x = harmonic(cell_mobility[:, :, :-1], cell_mobility[:, :, 1:])
    change_x = interior[:, :, :, 1:] - interior[:, :, :, :-1]
    self_block = self_block + gram_sum(change_x * conduct_x, change_x)
    conduct_y = harmonic(cell_mobility[:, :-1, :], cell_mobility[:, 1:, :])
    change_y = interior[:, :, 1:, :] - interior[:, :, :-1, :]
    self_block = self_block + gram_sum(change_y * conduct_y, change_y)
    conduct_z = vertical_ratio * harmonic(cell_mobility[:-1], cell_mobility[1:])
    change_z = interior[:, 1:] - interior[:, :-1]
    self_block = self_block + gram_sum(change_z * conduct_z, change_z)
    edges = (
        (interior[:, :, :, :1], padded_basis[:, :, 1:-1, :1], cell_mobility[:, :, :1], padded_mobility[:, 1:-1, :1]),
        (interior[:, :, :, -1:], padded_basis[:, :, 1:-1, -1:], cell_mobility[:, :, -1:], padded_mobility[:, 1:-1, -1:]),
        (interior[:, :, :1, :], padded_basis[:, :, :1, 1:-1], cell_mobility[:, :1, :], padded_mobility[:, :1, 1:-1]),
        (interior[:, :, -1:, :], padded_basis[:, :, -1:, 1:-1], cell_mobility[:, -1:, :], padded_mobility[:, -1:, 1:-1]),
    )
    side_blocks = []
    for edge_cells, ghost_cells, edge_mobility, ghost_mobility in edges:
        weighted = edge_cells * harmonic(edge_mobility, ghost_mobility)
        self_block = self_block + gram_sum(weighted, edge_cells)
        side_blocks.append(-gram_sum(weighted, ghost_cells))
    return jnp.stack([self_block] + side_blocks)


def coarse_apply(blocks, vector):
    padded = jnp.pad(vector, ((1, 1), (1, 1), (0, 0)))
    beside = jnp.stack([vector, padded[:-2, 1:-1], padded[2:, 1:-1], padded[1:-1, :-2], padded[1:-1, 2:]], axis=2)
    return jnp.einsum('abnkl,abnl->abk', blocks, beside, precision=lax.Precision.HIGHEST)


def coarse_solve(blocks, coarse_source):
    solution = jnp.zeros_like(coarse_source)
    remainder = coarse_source
    direction = coarse_source
    energy = jnp.sum(remainder * remainder)
    for iteration in range(ITERS):
        operator_image = coarse_apply(blocks, direction)
        step_length = energy / (jnp.sum(direction * operator_image) + epsilon)
        solution = solution + step_length * direction
        if iteration + 1 < ITERS:
            remainder = remainder - step_length * operator_image
            renewed = jnp.sum(remainder * remainder)
            direction = remainder + (renewed / (energy + epsilon)) * direction
            energy = renewed
    return solution


def reference(basis, mobility, accumulation, residual):
    padded_basis = jnp.pad(basis, ((0, 0), (0, 0), (1, 1), (1, 1)))
    padded_mobility = jnp.pad(mobility, ((0, 0), (1, 1), (1, 1)))

    def subdomain(number):
        along_x = number // N_GY
        along_y = number % N_GY
        start_y = (along_y * CY).astype(jnp.int32)
        start_x = (along_x * CX).astype(jnp.int32)
        anchor = jnp.zeros((), jnp.int32)
        window = lax.dynamic_slice(padded_basis, (anchor, anchor, start_y, start_x), (K, CZ, CY + 2, CX + 2)).astype(jnp.float32)
        beside_all = lax.dynamic_slice(padded_mobility, (anchor, start_y, start_x), (CZ, CY + 2, CX + 2)).astype(jnp.float32)
        storage = lax.dynamic_slice(accumulation, (anchor, start_y, start_x), (CZ, CY, CX))
        source = lax.dynamic_slice(residual, (anchor, start_y, start_x), (CZ, CY, CX))
        blocks = face_blocks(window, beside_all, storage)
        projected = jnp.einsum('kzyx,zyx->k', window[:, :, 1:-1, 1:-1], source, precision=lax.Precision.HIGHEST)
        return blocks, projected

    blocks, projected = lax.map(subdomain, jnp.arange(N_GX * N_GY, dtype=jnp.int32))
    blocks = blocks.reshape(N_GX, N_GY, 5, K, K)
    projected = projected.reshape(N_GX, N_GY, K)
    solution = coarse_solve(blocks, projected)
    expanded = basis.astype(jnp.float32).reshape(K, CZ, N_GY, CY, N_GX, CX)
    correction = jnp.einsum('kzbqap,abk->zbqap', expanded, solution, precision=lax.Precision.HIGHEST)
    return correction.reshape(CZ, NY, NX), solution
```

```python
import functools

import jax
import jax.numpy as jnp
from jax import lax
from jax.experimental import pallas as pl
from jax.experimental.pallas import tpu as pltpu
from jax.sharding import PartitionSpec as P


K = 16
EPS = 1e-06
VERTICAL = 0.1
MESH = pl.DeviceIdType.MESH
F32 = jnp.float32


def harmonic(a, b):
    return 2.0 * a * b / (a + b)


def lane_edges(x, lane, side):
    tiles = x.reshape(-1, 8, 128)
    out = jnp.zeros((8, 128), F32)
    for j in range(tiles.shape[0]):
        out = jnp.where(lane == j, tiles[j][:, side : side + 1], out)
    return out


def total(x):
    return jnp.sum(jnp.sum(x, axis=0, keepdims=True), axis=1, keepdims=True)


def kernel(
    nx, ny, basis_hbm, mob_hbm, acc_hbm, res_hbm, corr_ref, coarse_ref,
    basis, mob, acc, res, load_sem,
    coef, parts, zx, zy, hsend, ghost, hs_sem, hr_sem,
    row_a, slots_a, row_b, slots_b, ga_sem, gb_sem,
):
    gx, gy = lax.axis_index("gx"), lax.axis_index("gy")
    right, left = lax.rem(gx + 1, nx), lax.rem(gx + nx - 1, nx)
    above, below = lax.rem(gy + 1, ny), lax.rem(gy + ny - 1, ny)

    loads = [
        pltpu.make_async_copy(mob_hbm, mob, load_sem.at[0]),
        pltpu.make_async_copy(res_hbm, res, load_sem.at[1]),
        pltpu.make_async_copy(basis_hbm, basis, load_sem.at[2]),
        pltpu.make_async_copy(acc_hbm, acc, load_sem.at[3]),
    ]
    for c in loads:
        c.start()

    barrier = pltpu.get_barrier_semaphore()

    def greet_y(i, _):
        pl.semaphore_signal(barrier, 1, device_id=(gx, lax.rem(gy + i, ny)), device_id_type=MESH)
        return 0

    def greet_x(i, _):
        pl.semaphore_signal(barrier, 1, device_id=(lax.rem(gx + i, nx), gy), device_id_type=MESH)
        return 0

    lax.fori_loop(1, ny, greet_y, 0)
    lax.fori_loop(1, nx, greet_x, 0)

    lane = lax.broadcasted_iota(jnp.int32, (8, 128), 1)
    sub = lax.broadcasted_iota(jnp.int32, (8, 128), 0)
    cz, cy, cx = mob.shape

    loads[0].wait()
    m = mob[...].astype(F32)
    m_east, m_west = lane_edges(m, lane, cx - 1), lane_edges(m, lane, 0)
    for z in range(cz):
        hsend[0, 2, cz + z : cz + z + 1] = m[z, cy - 1 : cy]
        hsend[0, 3, cz + z : cz + z + 1] = m[z, 0:1]
    loads[1].wait()
    loads[2].wait()
    r = res[...]
    for k in range(K):
        parts[k] = jnp.sum((basis[k].astype(F32) * r).reshape(-1, 8, 128), axis=0)
    b = jnp.sum(jnp.sum(parts[...], axis=1), axis=1, keepdims=True)
    coef[0] = jnp.broadcast_to(b, (K, 128))

    def prolong(which):
        p = jnp.zeros((cz, cy, cx), F32)
        for k in range(K):
            p = p + basis[k].astype(F32) * coef[which, k : k + 1].reshape(1, 1, 128)
        return p

    p0 = prolong(0)
    p0_east, p0_west = lane_edges(p0, lane, cx - 1), lane_edges(p0, lane, 0)
    shifted = (lane >= 16) & (lane < 32)
    hsend[0, 0] = jnp.where(shifted, pltpu.roll(m_east, 16, 1), p0_east)
    hsend[0, 1] = jnp.where(shifted, pltpu.roll(m_west, 16, 1), p0_west)
    for z in range(cz):
        hsend[0, 2, z : z + 1] = p0[z, cy - 1 : cy]
        hsend[0, 3, z : z + 1] = p0[z, 0:1]

    pl.semaphore_wait(barrier, nx + ny - 2)

    def halo(step):
        to = [(right, gy), (left, gy), (gx, above), (gx, below)]
        return [
            pltpu.make_async_remote_copy(
                hsend.at[step, s], ghost.at[step, s ^ 1],
                hs_sem.at[step, s], hr_sem.at[step, s ^ 1],
                device_id=to[s], device_id_type=MESH,
            )
            for s in range(4)
        ]

    first = halo(0)
    for c in first:
        c.start()

    tx = harmonic(m, pltpu.roll(m, cx - 1, 2))
    lane3 = lax.broadcasted_iota(jnp.int32, (cz, cy, cx), 2)
    row3 = lax.broadcasted_iota(jnp.int32, (cz, cy, cx), 1)
    tx = jnp.where(lane3 == cx - 1, 0.0, tx)
    ty = jnp.where(row3 == cy - 1, 0.0, harmonic(m, pltpu.roll(m, cy - 1, 1)))
    tz = VERTICAL * harmonic(m[:-1], m[1:])
    loads[3].wait()
    ac = acc[...]

    def differences(p):
        return p - pltpu.roll(p, cx - 1, 2), p - pltpu.roll(p, cy - 1, 1), p[:-1] - p[1:]

    d0x, d0y, d0z = differences(p0)
    fx, fy, fz = tx * d0x, ty * d0y, tz * d0z
    jp = ac * p0 + (fx - pltpu.roll(fx, 1, 2)) + (fy - pltpu.roll(fy, 1, 1))
    none = jnp.zeros((1, cy, cx), F32)
    jp = jp + jnp.concatenate([fz, none], axis=0) - jnp.concatenate([none, fz], axis=0)
    for k in range(K):
        zk = basis[k].astype(F32)
        parts[k] = jnp.sum((zk * jp).reshape(-1, 8, 128), axis=0)
        zx[k, 0] = lane_edges(zk, lane, cx - 1)
        zx[k, 1] = lane_edges(zk, lane, 0)
        zero = jnp.zeros((cz, 128), F32)
        zy[k, 0] = jnp.concatenate([zk[z, cy - 1 : cy] for z in range(cz)] + [zero], axis=0)
        zy[k, 1] = jnp.concatenate([zk[z, 0:1] for z in range(cz)] + [zero], axis=0)

    has = [gx < nx - 1, gx > 0, gy < ny - 1, gy > 0]
    edge_p0 = [p0_east, p0_west, hsend[0, 2], hsend[0, 3]]

    for c in first:
        c.wait_recv()
    t_edge, flux = [], []
    for s in range(4):
        g = ghost[0, s]
        if s < 2:
            mine, other = (m_east, m_west)[s], pltpu.roll(g, 128 - 16, 1)
            inside = lane < 16
        else:
            mine, other = pltpu.roll(edge_p0[s], 8 - cz, 0), pltpu.roll(g, 8 - cz, 0)
            inside = sub < cz
        t = jnp.where(inside & has[s], harmonic(mine, other), 0.0)
        t_edge.append(t)
        flux.append(t * (edge_p0[s] - g))
    for k in range(K):
        parts[k] = parts[k] + (zx[k, 0] * flux[0] + zx[k, 1] * flux[1]) + (
            zy[k, 0] * flux[2] + zy[k, 1] * flux[3]
        )
    q = jnp.sum(jnp.sum(parts[...], axis=1), axis=1, keepdims=True)
    coef[1] = jnp.broadcast_to(q, (K, 128))

    edge_p1 = [jnp.zeros((8, 128), F32) for _ in range(4)]
    for k in range(K):
        qk = coef[1, k : k + 1]
        edge_p1[0] = edge_p1[0] + zx[k, 0] * qk
        edge_p1[1] = edge_p1[1] + zx[k, 1] * qk
        edge_p1[2] = edge_p1[2] + zy[k, 0] * qk
        edge_p1[3] = edge_p1[3] + zy[k, 1] * qk
    for s in range(4):
        hsend[1, s] = edge_p1[s]
    second = halo(1)
    for c in second:
        c.start()

    bv, qv = coef[0], coef[1]
    qq = jnp.sum(qv * qv, axis=0, keepdims=True)
    bq = jnp.sum(bv * qv, axis=0, keepdims=True)
    bb = jnp.sum(bv * bv, axis=0, keepdims=True)
    ratio = jnp.where(qq > 0.0, bq / jnp.where(qq > 0.0, qq, 1.0), 0.0)
    rest = bv - ratio * qv
    rr = jnp.sum(rest * rest, axis=0, keepdims=True)

    p1 = prolong(1)
    d1x, d1y, d1z = differences(p1)
    ratio3 = ratio.reshape(1, 1, 128)
    pr = p0 - ratio3 * p1
    rx, ry, rz = d0x - ratio3 * d1x, d0y - ratio3 * d1y, d0z - ratio3 * d1z

    def inside_energy(a, ax, ay, az, c, cxx, cyy, czz):
        e = ac * a * c + tx * ax * cxx + ty * ay * cyy
        return jnp.sum(e.reshape(-1, 8, 128), axis=0) + jnp.sum(
            (tz * az * czz).reshape(-1, 8, 128), axis=0
        )

    e_rr = inside_energy(pr, rx, ry, rz, pr, rx, ry, rz)
    e_rp = inside_energy(pr, rx, ry, rz, p1, d1x, d1y, d1z)
    e_pp = inside_energy(p1, d1x, d1y, d1z, p1, d1x, d1y, d1z)

    for c in second:
        c.wait_recv()
    for s in range(4):
        dp = edge_p1[s] - ghost[1, s]
        dr = (edge_p0[s] - ghost[0, s]) - ratio * dp
        half = 0.5 * t_edge[s]
        e_rr = e_rr + half * dr * dr
        e_rp = e_rp + half * dr * dp
        e_pp = e_pp + half * dp * dp

    lane1 = lax.broadcasted_iota(jnp.int32, (1, 128), 1)
    row = jnp.zeros((1, 128), F32)
    for i, v in enumerate([bb, bq, rr, ratio, qq, total(e_rr), total(e_rp), total(e_pp)]):
        row = jnp.where(lane1 == gy * 8 + i, v, row)
    row_a[...] = row

    def send_y(i, _):
        h = (i + 1) // 2
        far = ny // 2 + lax.rem(i, 2) * 2 * h - h
        pltpu.make_async_remote_copy(
            row_a, slots_a.at[gy], ga_sem.at[0], ga_sem.at[1],
            device_id=(gx, lax.rem(gy + far, ny)), device_id_type=MESH,
        ).start()
        return 0

    lax.fori_loop(0, ny - 1, send_y, 0)
    some = slots_a.at[pl.ds(0, ny - 1)]
    pltpu.make_async_copy(some, some, ga_sem.at[1]).wait()
    for i in range(ny):
        row = row + jnp.where(gy == i, 0.0, slots_a[i])
    row_b[...] = row

    def send_x(i, _):
        pltpu.make_async_remote_copy(
            row_b, slots_b.at[gx], gb_sem.at[0], gb_sem.at[1],
            device_id=(lax.rem(gx + i, nx), gy), device_id_type=MESH,
        ).start()
        return 0

    lax.fori_loop(1, nx, send_x, 0)
    some_b = slots_b.at[pl.ds(0, nx - 1)]
    pltpu.make_async_copy(some_b, some_b, gb_sem.at[1]).wait()
    every = jnp.concatenate(
        [jnp.where(gx == i, row, slots_b[i]) for i in range(nx)], axis=0
    )
    lanes = lax.rem(lax.broadcasted_iota(jnp.int32, (nx, 128), 1), 8)

    def over_all(x, i):
        return total(jnp.where(lanes == i, x, 0.0))

    energy = over_all(every, 0)
    step0 = energy / (over_all(every, 1) + EPS)
    next1, next2 = pltpu.roll(every, 127, 1), pltpu.roll(every, 126, 1)
    off = next1 - step0
    renewed = over_all(every + off * off * next2, 2)
    alpha = 1.0 + renewed / (energy + EPS)
    lean = alpha * pltpu.roll(every, 2, 1) - step0
    curved = alpha * alpha * every + lean * (2.0 * alpha * next1 + lean * next2)
    step1 = renewed / (over_all(curved, 5) + EPS)
    c0, c1 = step0 + step1 * alpha, -(step1 * step0)

    corr_ref[...] = c0.reshape(1, 1, 1) * p0 + c1.reshape(1, 1, 1) * p1
    x = c0 * coef[0] + c1 * coef[1]
    diag = lax.broadcasted_iota(jnp.int32, (K, 128), 0) == lax.broadcasted_iota(jnp.int32, (K, 128), 1)
    coarse_ref[0] = jnp.sum(jnp.where(diag, x, 0.0), axis=0, keepdims=True)[:, :K]

    for c in first + second:
        c.wait_send()
    pltpu.make_async_copy(some, some, ga_sem.at[0]).wait()
    pltpu.make_async_copy(some_b, some_b, gb_sem.at[0]).wait()


def solution(mesh):
    nx, ny = mesh.shape["gx"], mesh.shape["gy"]

    def per_device(basis, mobility, accumulation, residual):
        cells = mobility.shape
        vmem = pltpu.VMEM
        return pl.pallas_call(
            functools.partial(kernel, nx, ny),
            out_shape=(
                jax.ShapeDtypeStruct(cells, F32),
                jax.ShapeDtypeStruct((1, 1, K), F32),
            ),
            in_specs=[pl.BlockSpec(memory_space=pl.ANY)] * 4,
            out_specs=(pl.BlockSpec(memory_space=pltpu.VMEM),) * 2,
            scratch_shapes=[
                vmem(basis.shape, basis.dtype),
                vmem(cells, mobility.dtype),
                vmem(cells, F32),
                vmem(cells, F32),
                pltpu.SemaphoreType.DMA((4,)),
                vmem((2, K, 128), F32),
                vmem((K, 8, 128), F32),
                vmem((K, 2, 8, 128), F32),
                vmem((K, 2, 8, 128), F32),
                vmem((2, 4, 8, 128), F32),
                vmem((2, 4, 8, 128), F32),
                pltpu.SemaphoreType.DMA((2, 4)),
                pltpu.SemaphoreType.DMA((2, 4)),
                vmem((1, 128), F32),
                vmem((ny, 1, 128), F32),
                vmem((1, 128), F32),
                vmem((nx, 1, 128), F32),
                pltpu.SemaphoreType.DMA((2,)),
                pltpu.SemaphoreType.DMA((2,)),
            ],
            compiler_params=pltpu.CompilerParams(collective_id=0, has_side_effects=True),
        )(basis, mobility, accumulation, residual)

    cells = P(None, "gy", "gx")
    return jax.shard_map(
        per_device,
        mesh=mesh,
        in_specs=(P(None, None, "gy", "gx"), cells, cells, cells),
        out_specs=(cells, P("gx", "gy", None)),
        check_vma=False,
    )
```

```python
import functools

import jax
import jax.numpy as jnp
from jax import lax
from jax.experimental import pallas as pl
from jax.experimental.pallas import tpu as pltpu
from jax.sharding import PartitionSpec as P


K = 16
EPS = 1e-06
VERTICAL = 0.1
MESH = pl.DeviceIdType.MESH
F32 = jnp.float32


def harmonic(a, b):
    return 2.0 * a * b / (a + b)


def lane_edges(x, lane, side):
    tiles = x.reshape(-1, 8, 128)
    out = jnp.zeros((8, 128), F32)
    for j in range(tiles.shape[0]):
        out = jnp.where(lane == j, tiles[j][:, side : side + 1], out)
    return out


def total(x):
    return jnp.sum(jnp.sum(x, axis=0, keepdims=True), axis=1, keepdims=True)


def signal(sem, x, y):
    pl.semaphore_signal(sem, 1, device_id=(x, y), device_id_type=MESH)


def kernel(
    nx, ny, basis_hbm, mob_hbm, acc_hbm, res_hbm, field, small_ref,
    basis, mob, acc, res, load_sem,
    coef, parts, zx, zy, hsend, ghost, hs_sem, hr_sem,
    row_a, slots_a, row_b, slots_b, ga_sem, gb_sem,
    far_x, far_y, met,
):
    gx, gy = lax.axis_index("gx"), lax.axis_index("gy")
    chip, core = gx // 2, lax.rem(gx, 2)
    twin = gx + 1 - 2 * core
    right, left = lax.rem(gx + 1, nx), lax.rem(gx + nx - 1, nx)
    above, below = lax.rem(gy + 1, ny), lax.rem(gy + ny - 1, ny)

    loads = [
        pltpu.make_async_copy(mob_hbm, mob, load_sem.at[0]),
        pltpu.make_async_copy(res_hbm, res, load_sem.at[1]),
        pltpu.make_async_copy(basis_hbm, basis, load_sem.at[2]),
        pltpu.make_async_copy(acc_hbm, acc, load_sem.at[3]),
    ]
    for c in loads:
        c.start()

    barrier = pltpu.get_barrier_semaphore()
    for x, y in ((right, gy), (left, gy), (gx, above), (gx, below)):
        signal(barrier, x, y)

    reach_y = [d for d in (1, 2, 4, 8, 16, 32) if d < ny // 2]
    reach_x = [d for d in (1, 2, 4, 8, 16, 32) if d < nx // 2]

    def tell_y(i):
        if i < len(reach_y):
            signal(far_y.at[i], gx, lax.rem(gy + reach_y[i], ny))
            signal(far_y.at[i], gx, lax.rem(gy + ny - reach_y[i], ny))

    def tell_x(i):
        if i < len(reach_x):
            signal(far_x.at[i], lax.rem(gx + reach_x[i], nx), gy)
            signal(far_x.at[i], lax.rem(gx + nx - reach_x[i], nx), gy)

    def hear_y(i):
        if i < len(reach_y):
            pl.semaphore_wait(far_y.at[i], 2)

    def hear_x(i):
        if i < len(reach_x):
            pl.semaphore_wait(far_x.at[i], 2)

    lane = lax.broadcasted_iota(jnp.int32, (8, 128), 1)
    sub = lax.broadcasted_iota(jnp.int32, (8, 128), 0)
    cz, cy, cx = mob.shape

    loads[0].wait()
    m = mob[...].astype(F32)
    m_east, m_west = lane_edges(m, lane, cx - 1), lane_edges(m, lane, 0)
    for z in range(cz):
        hsend[0, 2, cz + z : cz + z + 1] = m[z, cy - 1 : cy]
        hsend[0, 3, cz + z : cz + z + 1] = m[z, 0:1]
    loads[1].wait()
    loads[2].wait()
    r = res[...]
    for k in range(K):
        parts[k] = jnp.sum((basis[k].astype(F32) * r).reshape(-1, 8, 128), axis=0)
    b = jnp.sum(jnp.sum(parts[...], axis=1), axis=1, keepdims=True)
    coef[0] = jnp.broadcast_to(b, (K, 128))

    def prolong(which):
        p = jnp.zeros((cz, cy, cx), F32)
        for k in range(K):
            p = p + basis[k].astype(F32) * coef[which, k : k + 1].reshape(1, 1, 128)
        return p

    p0 = prolong(0)
    p0_east, p0_west = lane_edges(p0, lane, cx - 1), lane_edges(p0, lane, 0)
    shifted = (lane >= 16) & (lane < 32)
    hsend[0, 0] = jnp.where(shifted, pltpu.roll(m_east, 16, 1), p0_east)
    hsend[0, 1] = jnp.where(shifted, pltpu.roll(m_west, 16, 1), p0_west)
    for z in range(cz):
        hsend[0, 2, z : z + 1] = p0[z, cy - 1 : cy]
        hsend[0, 3, z : z + 1] = p0[z, 0:1]

    pl.semaphore_wait(barrier, 4)

    def halo(step):
        to = [(right, gy), (left, gy), (gx, above), (gx, below)]
        return [
            pltpu.make_async_remote_copy(
                hsend.at[step, s], ghost.at[step, s ^ 1],
                hs_sem.at[step, s], hr_sem.at[step, s ^ 1],
                device_id=to[s], device_id_type=MESH,
            )
            for s in range(4)
        ]

    first = halo(0)
    for c in first:
        c.start()
    tell_y(0)
    tell_x(0)

    tx = harmonic(m, pltpu.roll(m, cx - 1, 2))
    lane3 = lax.broadcasted_iota(jnp.int32, (cz, cy, cx), 2)
    row3 = lax.broadcasted_iota(jnp.int32, (cz, cy, cx), 1)
    tx = jnp.where(lane3 == cx - 1, 0.0, tx)
    ty = jnp.where(row3 == cy - 1, 0.0, harmonic(m, pltpu.roll(m, cy - 1, 1)))
    tz = VERTICAL * harmonic(m[:-1], m[1:])
    loads[3].wait()
    ac = acc[...]

    def differences(p):
        return p - pltpu.roll(p, cx - 1, 2), p - pltpu.roll(p, cy - 1, 1), p[:-1] - p[1:]

    d0x, d0y, d0z = differences(p0)
    fx, fy, fz = tx * d0x, ty * d0y, tz * d0z
    jp = ac * p0 + (fx - pltpu.roll(fx, 1, 2)) + (fy - pltpu.roll(fy, 1, 1))
    none = jnp.zeros((1, cy, cx), F32)
    jp = jp + jnp.concatenate([fz, none], axis=0) - jnp.concatenate([none, fz], axis=0)
    for k in range(K):
        zk = basis[k].astype(F32)
        parts[k] = jnp.sum((zk * jp).reshape(-1, 8, 128), axis=0)
        zx[k, 0] = lane_edges(zk, lane, cx - 1)
        zx[k, 1] = lane_edges(zk, lane, 0)
        zero = jnp.zeros((cz, 128), F32)
        zy[k, 0] = jnp.concatenate([zk[z, cy - 1 : cy] for z in range(cz)] + [zero], axis=0)
        zy[k, 1] = jnp.concatenate([zk[z, 0:1] for z in range(cz)] + [zero], axis=0)

    field[0] = p0
    hear_y(0)
    tell_y(1)
    has = [gx < nx - 1, gx > 0, gy < ny - 1, gy > 0]
    edge_p0 = [p0_east, p0_west, hsend[0, 2], hsend[0, 3]]

    for c in first:
        c.wait_recv()
    hear_x(0)
    tell_x(1)
    t_edge, flux = [], []
    for s in range(4):
        g = ghost[0, s]
        if s < 2:
            mine, other = (m_east, m_west)[s], pltpu.roll(g, 128 - 16, 1)
            inside = lane < 16
        else:
            mine, other = pltpu.roll(edge_p0[s], 8 - cz, 0), pltpu.roll(g, 8 - cz, 0)
            inside = sub < cz
        t = jnp.where(inside & has[s], harmonic(mine, other), 0.0)
        t_edge.append(t)
        flux.append(t * (edge_p0[s] - g))
    for k in range(K):
        parts[k] = parts[k] + (zx[k, 0] * flux[0] + zx[k, 1] * flux[1]) + (
            zy[k, 0] * flux[2] + zy[k, 1] * flux[3]
        )
    q = jnp.sum(jnp.sum(parts[...], axis=1), axis=1, keepdims=True)
    coef[1] = jnp.broadcast_to(q, (K, 128))

    edge_p1 = [jnp.zeros((8, 128), F32) for _ in range(4)]
    for k in range(K):
        qk = coef[1, k : k + 1]
        edge_p1[0] = edge_p1[0] + zx[k, 0] * qk
        edge_p1[1] = edge_p1[1] + zx[k, 1] * qk
        edge_p1[2] = edge_p1[2] + zy[k, 0] * qk
        edge_p1[3] = edge_p1[3] + zy[k, 1] * qk
    for s in range(4):
        hsend[1, s] = edge_p1[s]
    second = halo(1)
    for c in second:
        c.start()
    hear_y(1)
    tell_y(2)

    bv, qv = coef[0], coef[1]
    qq = jnp.sum(qv * qv, axis=0, keepdims=True)
    bq = jnp.sum(bv * qv, axis=0, keepdims=True)
    bb = jnp.sum(bv * bv, axis=0, keepdims=True)
    ratio = jnp.where(qq > 0.0, bq / jnp.where(qq > 0.0, qq, 1.0), 0.0)
    rest = bv - ratio * qv
    rr = jnp.sum(rest * rest, axis=0, keepdims=True)

    p1 = prolong(1)
    field[1] = p1
    d1x, d1y, d1z = differences(p1)
    ratio3 = ratio.reshape(1, 1, 128)
    pr = p0 - ratio3 * p1
    rx, ry, rz = d0x - ratio3 * d1x, d0y - ratio3 * d1y, d0z - ratio3 * d1z

    def inside_energy(a, ax, ay, az, c, cxx, cyy, czz):
        e = ac * a * c + tx * ax * cxx + ty * ay * cyy
        return jnp.sum(e.reshape(-1, 8, 128), axis=0) + jnp.sum(
            (tz * az * czz).reshape(-1, 8, 128), axis=0
        )

    e_rr = inside_energy(pr, rx, ry, rz, pr, rx, ry, rz)
    e_rp = inside_energy(pr, rx, ry, rz, p1, d1x, d1y, d1z)
    e_pp = inside_energy(p1, d1x, d1y, d1z, p1, d1x, d1y, d1z)

    hear_y(2)
    signal(met, twin, gy)
    hear_x(1)
    tell_x(2)
    for c in second:
        c.wait_recv()
    for s in range(4):
        dp = edge_p1[s] - ghost[1, s]
        dr = (edge_p0[s] - ghost[0, s]) - ratio * dp
        half = 0.5 * t_edge[s]
        e_rr = e_rr + half * dr * dr
        e_rp = e_rp + half * dr * dp
        e_pp = e_pp + half * dp * dp

    lane1 = lax.broadcasted_iota(jnp.int32, (1, 128), 1)
    row = jnp.zeros((1, 128), F32)
    for i, v in enumerate([bb, bq, rr, ratio, qq, total(e_rr), total(e_rp), total(e_pp)]):
        row = jnp.where(lane1 == gy * 8 + i, v, row)
    row_a[...] = row
    pl.semaphore_wait(met, 1)

    def send_a(x, away):
        pltpu.make_async_remote_copy(
            row_a, slots_a.at[core * ny + gy], ga_sem.at[0], ga_sem.at[1],
            device_id=(x, lax.rem(gy + away, ny)), device_id_type=MESH,
        ).start()

    for away in sorted(range(1, ny), key=lambda d: -min(d, ny - d)):
        send_a(gx, away)
        send_a(twin, away)
    send_a(twin, 0)
    hear_x(2)
    tell_x(3)
    some = slots_a.at[pl.ds(0, 2 * ny - 1)]
    pltpu.make_async_copy(some, some, ga_sem.at[1]).wait()
    for c in range(2):
        both = jnp.zeros((1, 128), F32)
        for i in range(ny):
            both = both + jnp.where((core == c) & (gy == i), row, slots_a[c * ny + i])
        row_b[c] = both

    hear_x(3)
    chips = nx // 2
    ring_x = 4 if chips % 4 == 0 else chips
    ring_y = chips // ring_x
    cx0, cy0 = lax.rem(chip, ring_x), chip // ring_x

    def hops(d):
        return min(d[0], ring_x - d[0]) + min(d[1], ring_y - d[1])

    for dx, dy in sorted(
        ((i, j) for i in range(ring_x) for j in range(ring_y) if i + j), key=lambda d: -hops(d)
    ):
        to = lax.rem(cy0 + dy, ring_y) * ring_x + lax.rem(cx0 + dx, ring_x)
        pltpu.make_async_remote_copy(
            row_b, slots_b.at[chip], gb_sem.at[0], gb_sem.at[1],
            device_id=(to * 2 + core, gy), device_id_type=MESH,
        ).start()
    some_b = slots_b.at[pl.ds(0, chips - 1)]
    pltpu.make_async_copy(some_b, some_b, gb_sem.at[1]).wait()
    every = jnp.concatenate(
        [
            jnp.where(chip == i, row_b[c], slots_b[i, c])
            for i in range(chips)
            for c in range(2)
        ],
        axis=0,
    )
    lanes = lax.rem(lax.broadcasted_iota(jnp.int32, (nx, 128), 1), 8)

    def over_all(x, i):
        return total(jnp.where(lanes == i, x, 0.0))

    energy = over_all(every, 0)
    step0 = energy / (over_all(every, 1) + EPS)
    next1, next2 = pltpu.roll(every, 127, 1), pltpu.roll(every, 126, 1)
    off = next1 - step0
    renewed = over_all(every + off * off * next2, 2)
    alpha = 1.0 + renewed / (energy + EPS)
    lean = alpha * pltpu.roll(every, 2, 1) - step0
    curved = alpha * alpha * every + lean * (2.0 * alpha * next1 + lean * next2)
    step1 = renewed / (over_all(curved, 5) + EPS)
    c0, c1 = step0 + step1 * alpha, -(step1 * step0)

    x = c0 * coef[0] + c1 * coef[1]
    diag = lax.broadcasted_iota(jnp.int32, (K, 128), 0) == lax.broadcasted_iota(jnp.int32, (K, 128), 1)
    small_ref[0:1] = jnp.sum(jnp.where(diag, x, 0.0), axis=0, keepdims=True)
    small_ref[1:2] = jnp.broadcast_to(c0, (1, 128))
    small_ref[2:3] = jnp.broadcast_to(c1, (1, 128))

    for c in first + second:
        c.wait_send()
    pltpu.make_async_copy(some, some, ga_sem.at[0]).wait()
    pltpu.make_async_copy(some_b, some_b, gb_sem.at[0]).wait()


def solution(mesh):
    nx, ny = mesh.shape["gx"], mesh.shape["gy"]

    def per_device(basis, mobility, accumulation, residual):
        cells = mobility.shape
        vmem = pltpu.VMEM
        field, small = pl.pallas_call(
            functools.partial(kernel, nx, ny),
            out_shape=(
                vmem((2, *cells), F32),
                vmem((8, 128), F32),
            ),
            in_specs=[pl.BlockSpec(memory_space=pl.ANY)] * 4,
            out_specs=(pl.BlockSpec(memory_space=pltpu.VMEM),) * 2,
            scratch_shapes=[
                vmem(basis.shape, basis.dtype),
                vmem(cells, mobility.dtype),
                vmem(cells, F32),
                vmem(cells, F32),
                pltpu.SemaphoreType.DMA((4,)),
                vmem((2, K, 128), F32),
                vmem((K, 8, 128), F32),
                vmem((K, 2, 8, 128), F32),
                vmem((K, 2, 8, 128), F32),
                vmem((2, 4, 8, 128), F32),
                vmem((2, 4, 8, 128), F32),
                pltpu.SemaphoreType.DMA((2, 4)),
                pltpu.SemaphoreType.DMA((2, 4)),
                vmem((1, 128), F32),
                vmem((2 * ny, 1, 128), F32),
                vmem((2, 1, 128), F32),
                vmem((nx // 2, 2, 1, 128), F32),
                pltpu.SemaphoreType.DMA((2,)),
                pltpu.SemaphoreType.DMA((2,)),
                pltpu.SemaphoreType.REGULAR((4,)),
                pltpu.SemaphoreType.REGULAR((4,)),
                pltpu.SemaphoreType.REGULAR,
            ],
            compiler_params=pltpu.CompilerParams(collective_id=0, has_side_effects=True),
        )(basis, mobility, accumulation, residual)

        def finish(f, s, corr, coarse):
            corr[...] = s[1:2].reshape(1, 1, 128) * f[0] + s[2:3].reshape(1, 1, 128) * f[1]
            coarse[0] = s[0:1, :K]

        return pl.pallas_call(
            finish,
            out_shape=(jax.ShapeDtypeStruct(cells, F32), jax.ShapeDtypeStruct((1, 1, K), F32)),
            in_specs=[pl.BlockSpec(memory_space=pltpu.VMEM)] * 2,
        )(*(pltpu.with_memory_space_constraint(v, pltpu.VMEM) for v in (field, small)))

    cells = P(None, "gy", "gx")
    return jax.shard_map(
        per_device,
        mesh=mesh,
        in_specs=(P(None, None, "gy", "gx"), cells, cells, cells),
        out_specs=(cells, P("gx", "gy", None)),
        check_vma=False,
    )
```

```python
import functools

import jax
import jax.numpy as jnp
from jax import lax
from jax.experimental import pallas as pl
from jax.experimental.pallas import tpu as pltpu
from jax.sharding import PartitionSpec as P


K = 16
EPS = 1e-06
VERTICAL = 0.1
MESH = pl.DeviceIdType.MESH
F32 = jnp.float32


def harmonic(a, b):
    return 2.0 * a * b / (a + b)


def lane_edges(x, lane, side):
    tiles = x.reshape(-1, 8, 128)
    out = jnp.zeros((8, 128), F32)
    for j in range(tiles.shape[0]):
        out = jnp.where(lane == j, tiles[j][:, side : side + 1], out)
    return out


def total(x):
    return jnp.sum(jnp.sum(x, axis=0, keepdims=True), axis=1, keepdims=True)


def signal(sem, x, y):
    pl.semaphore_signal(sem, 1, device_id=(x, y), device_id_type=MESH)


def kernel(
    nx, ny, basis_hbm, mob_hbm, acc_hbm, res_hbm, field, small_ref,
    basis, mob, acc, res, load_sem,
    coef, parts, zx, zy, hsend, ghost, hs_sem, hr_sem,
    row_a, slots_a, row_b, slots_b, ga_sem, gb_sem,
    far_x, far_y, met,
):
    gx, gy = lax.axis_index("gx"), lax.axis_index("gy")
    chip, core = gx // 2, lax.rem(gx, 2)
    twin = gx + 1 - 2 * core
    right, left = gx + 1, gx - 1
    above, below = gy + 1, gy - 1

    quarters = [pl.ds(k, K // 4) for k in range(0, K, K // 4)]
    loads = [
        pltpu.make_async_copy(mob_hbm, mob, load_sem.at[0]),
        pltpu.make_async_copy(res_hbm, res, load_sem.at[1]),
        *(
            pltpu.make_async_copy(basis_hbm.at[part], basis.at[part], load_sem.at[2 + i])
            for i, part in enumerate(quarters)
        ),
        pltpu.make_async_copy(acc_hbm, acc, load_sem.at[6]),
    ]
    for c in loads:
        c.start()

    has = [gx < nx - 1, gx > 0, gy < ny - 1, gy > 0]
    barrier = pltpu.get_barrier_semaphore()
    near_y = [d for d in (1, -1, 2, -2) if 2 * abs(d) < ny]
    for d in near_y:
        signal(barrier, gx, lax.rem(gy + ny + d, ny))
    reach_y = [d for d in (2, 4, 8, 16, 32) if d < ny // 2]
    reach_x = [d for d in (1, 2, 4, 8, 16, 32) if d < nx]

    def signal_x(sem, d):
        @pl.when(gx + d < nx)
        def _():
            signal(sem, gx + d, gy)

        @pl.when(gx >= d)
        def _():
            signal(sem, gx - d, gy)

    def count_x(d):
        return jnp.where(gx + d < nx, 1, 0) + jnp.where(gx >= d, 1, 0)

    signal_x(barrier, 1)

    def tell_y(i):
        if i < len(reach_y):
            signal(far_y.at[i], gx, lax.rem(gy + reach_y[i], ny))
            signal(far_y.at[i], gx, lax.rem(gy + ny - reach_y[i], ny))

    def tell_x(i):
        if i < len(reach_x):
            signal_x(far_x.at[i], reach_x[i])

    def hear_y(i):
        if i < len(reach_y):
            pl.semaphore_wait(far_y.at[i], 2)

    def hear_x(i):
        if i < len(reach_x):
            pl.semaphore_wait(far_x.at[i], count_x(reach_x[i]))

    lane = lax.broadcasted_iota(jnp.int32, (8, 128), 1)
    sub = lax.broadcasted_iota(jnp.int32, (8, 128), 0)
    cz, cy, cx = mob.shape

    loads[0].wait()
    m = mob[...].astype(F32)
    m_east, m_west = lane_edges(m, lane, cx - 1), lane_edges(m, lane, 0)
    for z in range(cz):
        hsend[0, 2, cz + z : cz + z + 1] = m[z, cy - 1 : cy]
        hsend[0, 3, cz + z : cz + z + 1] = m[z, 0:1]
    loads[1].wait()
    r = res[...]
    for k in range(K):
        if k % (K // 4) == 0:
            loads[2 + k // (K // 4)].wait()
        parts[k] = jnp.sum((basis[k].astype(F32) * r).reshape(-1, 8, 128), axis=0)
    b = jnp.sum(jnp.sum(parts[...], axis=1), axis=1, keepdims=True)
    coef[0] = jnp.broadcast_to(b, (K, 128))

    def prolong(which):
        p = jnp.zeros((cz, cy, cx), F32)
        for k in range(K):
            p = p + basis[k].astype(F32) * coef[which, k : k + 1].reshape(1, 1, 128)
        return p

    p0 = prolong(0)
    p0_east, p0_west = lane_edges(p0, lane, cx - 1), lane_edges(p0, lane, 0)
    shifted = (lane >= 16) & (lane < 32)
    hsend[0, 0] = jnp.where(shifted, pltpu.roll(m_east, 16, 1), p0_east)
    hsend[0, 1] = jnp.where(shifted, pltpu.roll(m_west, 16, 1), p0_west)
    for z in range(cz):
        hsend[0, 2, z : z + 1] = p0[z, cy - 1 : cy]
        hsend[0, 3, z : z + 1] = p0[z, 0:1]

    pl.semaphore_wait(barrier, count_x(1) + len(near_y))

    def halo(step):
        to = [(right, gy), (left, gy), (gx, above), (gx, below)]
        return [
            pltpu.make_async_remote_copy(
                hsend.at[step, s], ghost.at[step, s ^ 1],
                hs_sem.at[step, s], hr_sem.at[step, s ^ 1],
                device_id=to[s], device_id_type=MESH,
            )
            for s in range(4)
        ]

    middle = ny // 2
    weighs = [has[0], gx < 0, has[2] & (gy < middle), has[3] & (gy > middle)]
    gives = [gx < 0, has[1], has[2] & (gy >= middle), has[3] & (gy <= middle)]

    def arrive(step, sides):
        for s in range(4):

            @pl.when(sides[s])
            def _(s=s):
                here = ghost.at[step, s]
                pltpu.make_async_copy(here, here, hr_sem.at[step, s]).wait()

    def each(copies, sides, act):
        for s in range(4):

            @pl.when(sides[s])
            def _(c=copies[s]):
                act(c)

    first = halo(0)
    each(first, has, lambda c: c.start())
    tell_y(0)
    tell_x(0)

    tx = harmonic(m, pltpu.roll(m, cx - 1, 2))
    lane3 = lax.broadcasted_iota(jnp.int32, (cz, cy, cx), 2)
    row3 = lax.broadcasted_iota(jnp.int32, (cz, cy, cx), 1)
    tx = jnp.where(lane3 == cx - 1, 0.0, tx)
    ty = jnp.where(row3 == cy - 1, 0.0, harmonic(m, pltpu.roll(m, cy - 1, 1)))
    tz = VERTICAL * harmonic(m[:-1], m[1:])
    loads[6].wait()
    ac = acc[...]

    def differences(p):
        return p - pltpu.roll(p, cx - 1, 2), p - pltpu.roll(p, cy - 1, 1), p[:-1] - p[1:]

    d0x, d0y, d0z = differences(p0)
    fx, fy, fz = tx * d0x, ty * d0y, tz * d0z
    jp = ac * p0 + (fx - pltpu.roll(fx, 1, 2)) + (fy - pltpu.roll(fy, 1, 1))
    none = jnp.zeros((1, cy, cx), F32)
    jp = jp + jnp.concatenate([fz, none], axis=0) - jnp.concatenate([none, fz], axis=0)
    for k in range(K):
        zk = basis[k].astype(F32)
        parts[k] = jnp.sum((zk * jp).reshape(-1, 8, 128), axis=0)
        zx[k, 0] = lane_edges(zk, lane, cx - 1)
        zx[k, 1] = lane_edges(zk, lane, 0)
        zero = jnp.zeros((cz, 128), F32)
        zy[k, 0] = jnp.concatenate([zk[z, cy - 1 : cy] for z in range(cz)] + [zero], axis=0)
        zy[k, 1] = jnp.concatenate([zk[z, 0:1] for z in range(cz)] + [zero], axis=0)

    field[0] = p0
    hear_y(0)
    tell_y(1)
    hear_x(0)
    tell_x(1)
    edge_p0 = [p0_east, p0_west, hsend[0, 2], hsend[0, 3]]

    arrive(0, has)
    t_edge, jump, flux = [], [], []
    for s in range(4):
        g = ghost[0, s]
        if s < 2:
            mine, other = (m_east, m_west)[s], pltpu.roll(g, 128 - 16, 1)
            inside = lane < 16
        else:
            mine, other = pltpu.roll(edge_p0[s], 8 - cz, 0), pltpu.roll(g, 8 - cz, 0)
            inside = sub < cz
        joined = inside & has[s]
        t = jnp.where(joined, harmonic(mine, other), 0.0)
        d = jnp.where(joined, edge_p0[s] - g, 0.0)
        t_edge.append((joined, t))
        jump.append(d)
        flux.append(t * d)
    for k in range(K):
        parts[k] = parts[k] + (zx[k, 0] * flux[0] + zx[k, 1] * flux[1]) + (
            zy[k, 0] * flux[2] + zy[k, 1] * flux[3]
        )
    q = jnp.sum(jnp.sum(parts[...], axis=1), axis=1, keepdims=True)
    coef[1] = jnp.broadcast_to(q, (K, 128))

    edge_p1 = [jnp.zeros((8, 128), F32) for _ in range(4)]
    for k in range(K):
        qk = coef[1, k : k + 1]
        edge_p1[0] = edge_p1[0] + zx[k, 0] * qk
        edge_p1[1] = edge_p1[1] + zx[k, 1] * qk
        edge_p1[2] = edge_p1[2] + zy[k, 0] * qk
        edge_p1[3] = edge_p1[3] + zy[k, 1] * qk
    for s in range(4):
        hsend[1, s] = edge_p1[s]
    second = halo(1)
    each(second, gives, lambda c: c.start())

    bv, qv = coef[0], coef[1]
    qq = jnp.sum(qv * qv, axis=0, keepdims=True)
    bq = jnp.sum(bv * qv, axis=0, keepdims=True)
    bb = jnp.sum(bv * bv, axis=0, keepdims=True)
    ratio = jnp.where(qq > 0.0, bq / jnp.where(qq > 0.0, qq, 1.0), 0.0)
    rest = bv - ratio * qv
    rr = jnp.sum(rest * rest, axis=0, keepdims=True)

    p1 = prolong(1)
    field[1] = p1
    d1x, d1y, d1z = differences(p1)
    ratio3 = ratio.reshape(1, 1, 128)
    pr = p0 - ratio3 * p1
    rx, ry, rz = d0x - ratio3 * d1x, d0y - ratio3 * d1y, d0z - ratio3 * d1z

    def inside_energy(a, ax, ay, az, c, cxx, cyy, czz):
        e = ac * a * c + tx * ax * cxx + ty * ay * cyy
        return jnp.sum(e.reshape(-1, 8, 128), axis=0) + jnp.sum(
            (tz * az * czz).reshape(-1, 8, 128), axis=0
        )

    e_rr = inside_energy(pr, rx, ry, rz, pr, rx, ry, rz)
    e_rp = inside_energy(pr, rx, ry, rz, p1, d1x, d1y, d1z)
    e_pp = inside_energy(p1, d1x, d1y, d1z, p1, d1x, d1y, d1z)

    hear_y(1)
    signal(met, twin, gy)
    hear_x(1)
    tell_x(2)
    arrive(1, weighs)
    for s in (0, 2, 3):
        joined, t = t_edge[s]
        mine = joined & weighs[s]
        dp = jnp.where(mine, edge_p1[s] - ghost[1, s], 0.0)
        dr = jump[s] - ratio * dp
        t = jnp.where(mine, t, 0.0)
        e_rr = e_rr + t * dr * dr
        e_rp = e_rp + t * dr * dp
        e_pp = e_pp + t * dp * dp

    lane1 = lax.broadcasted_iota(jnp.int32, (1, 128), 1)
    row = jnp.zeros((1, 128), F32)
    for i, v in enumerate([bb, bq, rr, ratio, qq, total(e_rr), total(e_rp), total(e_pp)]):
        row = jnp.where(lane1 == gy * 8 + i, v, row)
    row_a[...] = row
    pl.semaphore_wait(met, 1)

    def send_a(x, away):
        pltpu.make_async_remote_copy(
            row_a, slots_a.at[core * ny + gy], ga_sem.at[0], ga_sem.at[1],
            device_id=(x, lax.rem(gy + away, ny)), device_id_type=MESH,
        ).start()

    for away in sorted(range(1, ny), key=lambda d: -min(d, ny - d)):
        send_a(gx, away)
        send_a(twin, away)
    send_a(twin, 0)
    hear_x(2)
    tell_x(3)
    hear_x(3)
    tell_x(4)
    some = slots_a.at[pl.ds(0, 2 * ny - 1)]
    each(first, has, lambda c: c.wait_send())
    each(second, gives, lambda c: c.wait_send())
    pltpu.make_async_copy(some, some, ga_sem.at[1]).wait()
    for c in range(2):
        both = jnp.zeros((1, 128), F32)
        for i in range(ny):
            both = both + jnp.where((core == c) & (gy == i), row, slots_a[c * ny + i])
        row_b[c] = both

    hear_x(4)
    chips = nx // 2
    ring_x = 4 if chips % 4 == 0 else chips
    ring_y = chips // ring_x
    cx0, cy0 = lax.rem(chip, ring_x), chip // ring_x

    def hops(d):
        return min(d[0], ring_x - d[0]) + min(d[1], ring_y - d[1])

    for dx, dy in sorted(
        ((i, j) for i in range(ring_x) for j in range(ring_y) if i + j), key=lambda d: -hops(d)
    ):
        to = lax.rem(cy0 + dy, ring_y) * ring_x + lax.rem(cx0 + dx, ring_x)
        pltpu.make_async_remote_copy(
            row_b, slots_b.at[chip], gb_sem.at[0], gb_sem.at[1],
            device_id=(to * 2 + core, gy), device_id_type=MESH,
        ).start()
    some_b = slots_b.at[pl.ds(0, chips - 1)]
    pltpu.make_async_copy(some, some, ga_sem.at[0]).wait()
    pltpu.make_async_copy(some_b, some_b, gb_sem.at[1]).wait()
    every = jnp.concatenate(
        [
            jnp.where(chip == i, row_b[c], slots_b[i, c])
            for i in range(chips)
            for c in range(2)
        ],
        axis=0,
    )
    lanes = lax.rem(lax.broadcasted_iota(jnp.int32, (nx, 128), 1), 8)

    def over_all(x, i):
        return total(jnp.where(lanes == i, x, 0.0))

    energy = over_all(every, 0)
    step0 = energy / (over_all(every, 1) + EPS)
    next1, next2 = pltpu.roll(every, 127, 1), pltpu.roll(every, 126, 1)
    off = next1 - step0
    renewed = over_all(every + off * off * next2, 2)
    alpha = 1.0 + renewed / (energy + EPS)
    lean = alpha * pltpu.roll(every, 2, 1) - step0
    curved = alpha * alpha * every + lean * (2.0 * alpha * next1 + lean * next2)
    step1 = renewed / (over_all(curved, 5) + EPS)
    c0, c1 = step0 + step1 * alpha, -(step1 * step0)

    x = c0 * coef[0] + c1 * coef[1]
    diag = lax.broadcasted_iota(jnp.int32, (K, 128), 0) == lax.broadcasted_iota(jnp.int32, (K, 128), 1)
    small_ref[0:1] = jnp.sum(jnp.where(diag, x, 0.0), axis=0, keepdims=True)
    small_ref[1:2] = jnp.broadcast_to(c0, (1, 128))
    small_ref[2:3] = jnp.broadcast_to(c1, (1, 128))

    pltpu.make_async_copy(some_b, some_b, gb_sem.at[0]).wait()


def solution(mesh):
    nx, ny = mesh.shape["gx"], mesh.shape["gy"]

    def per_device(basis, mobility, accumulation, residual):
        cells = mobility.shape
        vmem = pltpu.VMEM
        field, small = pl.pallas_call(
            functools.partial(kernel, nx, ny),
            out_shape=(
                vmem((2, *cells), F32),
                vmem((8, 128), F32),
            ),
            in_specs=[pl.BlockSpec(memory_space=pl.ANY)] * 4,
            out_specs=(pl.BlockSpec(memory_space=pltpu.VMEM),) * 2,
            scratch_shapes=[
                vmem(basis.shape, basis.dtype),
                vmem(cells, mobility.dtype),
                vmem(cells, F32),
                vmem(cells, F32),
                pltpu.SemaphoreType.DMA((7,)),
                vmem((2, K, 128), F32),
                vmem((K, 8, 128), F32),
                vmem((K, 2, 8, 128), F32),
                vmem((K, 2, 8, 128), F32),
                vmem((2, 4, 8, 128), F32),
                vmem((2, 4, 8, 128), F32),
                pltpu.SemaphoreType.DMA((2, 4)),
                pltpu.SemaphoreType.DMA((2, 4)),
                vmem((1, 128), F32),
                vmem((2 * ny, 1, 128), F32),
                vmem((2, 1, 128), F32),
                vmem((nx // 2, 2, 1, 128), F32),
                pltpu.SemaphoreType.DMA((2,)),
                pltpu.SemaphoreType.DMA((2,)),
                pltpu.SemaphoreType.REGULAR((5,)),
                pltpu.SemaphoreType.REGULAR((2,)),
                pltpu.SemaphoreType.REGULAR,
            ],
            compiler_params=pltpu.CompilerParams(collective_id=0, has_side_effects=True),
        )(basis, mobility, accumulation, residual)

        def finish(f, s, corr, coarse):
            corr[...] = s[1:2].reshape(1, 1, 128) * f[0] + s[2:3].reshape(1, 1, 128) * f[1]
            coarse[0] = s[0:1, :K]

        return pl.pallas_call(
            finish,
            out_shape=(jax.ShapeDtypeStruct(cells, F32), jax.ShapeDtypeStruct((1, 1, K), F32)),
            in_specs=[pl.BlockSpec(memory_space=pltpu.VMEM)] * 2,
        )(*(pltpu.with_memory_space_constraint(v, pltpu.VMEM) for v in (field, small)))

    cells = P(None, "gy", "gx")
    return jax.shard_map(
        per_device,
        mesh=mesh,
        in_specs=(P(None, None, "gy", "gx"), cells, cells, cells),
        out_specs=(cells, P("gx", "gy", None)),
        check_vma=False,
    )
```

```python
import functools

import jax
import jax.numpy as jnp
from jax import lax
from jax.experimental import pallas as pl
from jax.experimental.pallas import tpu as pltpu
from jax.sharding import PartitionSpec as P


K = 16
EPS = 1e-06
VERTICAL = 0.1
MESH = pl.DeviceIdType.MESH
F32 = jnp.float32


def harmonic(a, b):
    return 2.0 * a * b / (a + b)


def lane_edges(x, lane, side):
    tiles = x.reshape(-1, 8, 128)
    out = jnp.zeros((8, 128), F32)
    for j in range(tiles.shape[0]):
        out = jnp.where(lane == j, tiles[j][:, side : side + 1], out)
    return out


def total(x):
    return jnp.sum(jnp.sum(x, axis=0, keepdims=True), axis=1, keepdims=True)


def signal(sem, x, y):
    pl.semaphore_signal(sem, 1, device_id=(x, y), device_id_type=MESH)


def kernel(
    nx, ny, basis_hbm, mob_hbm, acc_hbm, res_hbm, field, small_ref,
    basis, mob, acc, res, load_sem,
    coef, parts, zx, zy, hsend, ghost, hs_sem, hr_sem,
    row_a, slots_a, row_b, slots_b, ga_sem, gb_sem,
    far_x, far_y, met,
):
    gx, gy = lax.axis_index("gx"), lax.axis_index("gy")
    chip, core = gx // 2, lax.rem(gx, 2)
    twin = gx + 1 - 2 * core
    right, left = lax.rem(gx + 1, nx), lax.rem(gx + nx - 1, nx)
    above, below = lax.rem(gy + 1, ny), lax.rem(gy + ny - 1, ny)

    quarters = [pl.ds(k, K // 4) for k in range(0, K, K // 4)]
    loads = [
        pltpu.make_async_copy(mob_hbm, mob, load_sem.at[0]),
        pltpu.make_async_copy(res_hbm, res, load_sem.at[1]),
        *(
            pltpu.make_async_copy(basis_hbm.at[part], basis.at[part], load_sem.at[2 + i])
            for i, part in enumerate(quarters)
        ),
        pltpu.make_async_copy(acc_hbm, acc, load_sem.at[6]),
    ]
    for c in loads:
        c.start()

    has = [gx < nx - 1, gx > 0, gy < ny - 1, gy > 0]
    barrier = pltpu.get_barrier_semaphore()
    near_y = [d for d in (1, -1, 2, -2) if 2 * abs(d) < ny]
    for d in near_y:
        signal(barrier, gx, lax.rem(gy + ny + d, ny))
    reach_y = [d for d in (2, 4, 8, 16, 32) if d < ny // 2]
    reach_x = [d for d in (1, 2, 4, 8, 16, 32) if d < nx]

    def signal_x(sem, d):
        @pl.when(gx + d < nx)
        def _():
            signal(sem, lax.rem(gx + d, nx), gy)

        @pl.when(gx >= d)
        def _():
            signal(sem, lax.rem(gx + nx - d, nx), gy)

    def count_x(d):
        return jnp.where(gx + d < nx, 1, 0) + jnp.where(gx >= d, 1, 0)

    signal_x(barrier, 1)

    def tell_y(i):
        if i < len(reach_y):
            signal(far_y.at[i], gx, lax.rem(gy + reach_y[i], ny))
            signal(far_y.at[i], gx, lax.rem(gy + ny - reach_y[i], ny))

    def tell_x(i):
        if i < len(reach_x):
            signal_x(far_x.at[i], reach_x[i])

    def hear_y(i):
        if i < len(reach_y):
            pl.semaphore_wait(far_y.at[i], 2)

    def hear_x(i):
        if i < len(reach_x):
            pl.semaphore_wait(far_x.at[i], count_x(reach_x[i]))

    lane = lax.broadcasted_iota(jnp.int32, (8, 128), 1)
    sub = lax.broadcasted_iota(jnp.int32, (8, 128), 0)
    cz, cy, cx = mob.shape

    loads[0].wait()
    m = mob[...].astype(F32)
    m_east, m_west = lane_edges(m, lane, cx - 1), lane_edges(m, lane, 0)
    for z in range(cz):
        hsend[0, 2, cz + z : cz + z + 1] = m[z, cy - 1 : cy]
        hsend[0, 3, cz + z : cz + z + 1] = m[z, 0:1]
    loads[1].wait()
    r = res[...]
    for k in range(K):
        if k % (K // 4) == 0:
            loads[2 + k // (K // 4)].wait()
        parts[k] = jnp.sum((basis[k].astype(F32) * r).reshape(-1, 8, 128), axis=0)
    b = jnp.sum(jnp.sum(parts[...], axis=1), axis=1, keepdims=True)
    coef[0] = jnp.broadcast_to(b, (K, 128))

    def prolong(which):
        p = jnp.zeros((cz, cy, cx), F32)
        for k in range(K):
            p = p + basis[k].astype(F32) * coef[which, k : k + 1].reshape(1, 1, 128)
        return p

    p0 = prolong(0)
    p0_east, p0_west = lane_edges(p0, lane, cx - 1), lane_edges(p0, lane, 0)
    shifted = (lane >= 16) & (lane < 32)
    hsend[0, 0] = jnp.where(shifted, pltpu.roll(m_east, 16, 1), p0_east)
    hsend[0, 1] = jnp.where(shifted, pltpu.roll(m_west, 16, 1), p0_west)
    for z in range(cz):
        hsend[0, 2, z : z + 1] = p0[z, cy - 1 : cy]
        hsend[0, 3, z : z + 1] = p0[z, 0:1]

    pl.semaphore_wait(barrier, count_x(1) + len(near_y))

    def halo(step):
        to = [(right, gy), (left, gy), (gx, above), (gx, below)]
        return [
            pltpu.make_async_remote_copy(
                hsend.at[step, s], ghost.at[step, s ^ 1],
                hs_sem.at[step, s], hr_sem.at[step, s ^ 1],
                device_id=to[s], device_id_type=MESH,
            )
            for s in range(4)
        ]

    middle = ny // 2
    weighs = [has[0], gx < 0, has[2] & (gy < middle), has[3] & (gy > middle)]
    gives = [gx < 0, has[1], has[2] & (gy >= middle), has[3] & (gy <= middle)]

    def arrive(step, sides):
        for s in range(4):

            @pl.when(sides[s])
            def _(s=s):
                here = ghost.at[step, s]
                pltpu.make_async_copy(here, here, hr_sem.at[step, s]).wait()

    def each(copies, sides, act):
        for s in range(4):

            @pl.when(sides[s])
            def _(c=copies[s]):
                act(c)

    first = halo(0)
    each(first, has, lambda c: c.start())
    tell_y(0)
    tell_x(0)

    tx = harmonic(m, pltpu.roll(m, cx - 1, 2))
    lane3 = lax.broadcasted_iota(jnp.int32, (cz, cy, cx), 2)
    row3 = lax.broadcasted_iota(jnp.int32, (cz, cy, cx), 1)
    tx = jnp.where(lane3 == cx - 1, 0.0, tx)
    ty = jnp.where(row3 == cy - 1, 0.0, harmonic(m, pltpu.roll(m, cy - 1, 1)))
    tz = VERTICAL * harmonic(m[:-1], m[1:])
    loads[6].wait()
    ac = acc[...]

    def differences(p):
        return p - pltpu.roll(p, cx - 1, 2), p - pltpu.roll(p, cy - 1, 1), p[:-1] - p[1:]

    d0x, d0y, d0z = differences(p0)
    fx, fy, fz = tx * d0x, ty * d0y, tz * d0z
    jp = ac * p0 + (fx - pltpu.roll(fx, 1, 2)) + (fy - pltpu.roll(fy, 1, 1))
    none = jnp.zeros((1, cy, cx), F32)
    jp = jp + jnp.concatenate([fz, none], axis=0) - jnp.concatenate([none, fz], axis=0)
    for k in range(K):
        zk = basis[k].astype(F32)
        parts[k] = jnp.sum((zk * jp).reshape(-1, 8, 128), axis=0)
        zx[k, 0] = lane_edges(zk, lane, cx - 1)
        zx[k, 1] = lane_edges(zk, lane, 0)
        zero = jnp.zeros((cz, 128), F32)
        zy[k, 0] = jnp.concatenate([zk[z, cy - 1 : cy] for z in range(cz)] + [zero], axis=0)
        zy[k, 1] = jnp.concatenate([zk[z, 0:1] for z in range(cz)] + [zero], axis=0)

    field[0] = p0
    hear_y(0)
    tell_y(1)
    hear_x(0)
    tell_x(1)
    edge_p0 = [p0_east, p0_west, hsend[0, 2], hsend[0, 3]]

    arrive(0, has)
    t_edge, jump, flux = [], [], []
    for s in range(4):
        g = ghost[0, s]
        if s < 2:
            mine, other = (m_east, m_west)[s], pltpu.roll(g, 128 - 16, 1)
            inside = lane < 16
        else:
            mine, other = pltpu.roll(edge_p0[s], 8 - cz, 0), pltpu.roll(g, 8 - cz, 0)
            inside = sub < cz
        joined = inside & has[s]
        t = jnp.where(joined, harmonic(mine, other), 0.0)
        d = jnp.where(joined, edge_p0[s] - g, 0.0)
        t_edge.append((joined, t))
        jump.append(d)
        flux.append(t * d)
    for k in range(K):
        parts[k] = parts[k] + (zx[k, 0] * flux[0] + zx[k, 1] * flux[1]) + (
            zy[k, 0] * flux[2] + zy[k, 1] * flux[3]
        )
    q = jnp.sum(jnp.sum(parts[...], axis=1), axis=1, keepdims=True)
    coef[1] = jnp.broadcast_to(q, (K, 128))

    edge_p1 = [jnp.zeros((8, 128), F32) for _ in range(4)]
    for k in range(K):
        qk = coef[1, k : k + 1]
        edge_p1[0] = edge_p1[0] + zx[k, 0] * qk
        edge_p1[1] = edge_p1[1] + zx[k, 1] * qk
        edge_p1[2] = edge_p1[2] + zy[k, 0] * qk
        edge_p1[3] = edge_p1[3] + zy[k, 1] * qk
    for s in range(4):
        hsend[1, s] = edge_p1[s]
    second = halo(1)
    each(second, gives, lambda c: c.start())

    bv, qv = coef[0], coef[1]
    qq = jnp.sum(qv * qv, axis=0, keepdims=True)
    bq = jnp.sum(bv * qv, axis=0, keepdims=True)
    bb = jnp.sum(bv * bv, axis=0, keepdims=True)
    ratio = jnp.where(qq > 0.0, bq / jnp.where(qq > 0.0, qq, 1.0), 0.0)
    rest = bv - ratio * qv
    rr = jnp.sum(rest * rest, axis=0, keepdims=True)

    p1 = prolong(1)
    field[1] = p1
    d1x, d1y, d1z = differences(p1)
    ratio3 = ratio.reshape(1, 1, 128)
    pr = p0 - ratio3 * p1
    rx, ry, rz = d0x - ratio3 * d1x, d0y - ratio3 * d1y, d0z - ratio3 * d1z

    def inside_energy(a, ax, ay, az, c, cxx, cyy, czz):
        e = ac * a * c + tx * ax * cxx + ty * ay * cyy
        return jnp.sum(e.reshape(-1, 8, 128), axis=0) + jnp.sum(
            (tz * az * czz).reshape(-1, 8, 128), axis=0
        )

    e_rr = inside_energy(pr, rx, ry, rz, pr, rx, ry, rz)
    e_rp = inside_energy(pr, rx, ry, rz, p1, d1x, d1y, d1z)
    e_pp = inside_energy(p1, d1x, d1y, d1z, p1, d1x, d1y, d1z)

    hear_y(1)
    signal(met, twin, gy)
    hear_x(1)
    tell_x(2)
    arrive(1, weighs)
    for s in (0, 2, 3):
        joined, t = t_edge[s]
        mine = joined & weighs[s]
        dp = jnp.where(mine, edge_p1[s] - ghost[1, s], 0.0)
        dr = jump[s] - ratio * dp
        t = jnp.where(mine, t, 0.0)
        e_rr = e_rr + t * dr * dr
        e_rp = e_rp + t * dr * dp
        e_pp = e_pp + t * dp * dp

    lane1 = lax.broadcasted_iota(jnp.int32, (1, 128), 1)
    row = jnp.zeros((1, 128), F32)
    for i, v in enumerate([bb, bq, rr, ratio, qq, total(e_rr), total(e_rp), total(e_pp)]):
        row = jnp.where(lane1 == gy * 8 + i, v, row)
    row_a[...] = row
    pl.semaphore_wait(met, 1)

    def send_a(x, away):
        pltpu.make_async_remote_copy(
            row_a, slots_a.at[core * ny + gy], ga_sem.at[0], ga_sem.at[1],
            device_id=(x, lax.rem(gy + away, ny)), device_id_type=MESH,
        ).start()

    for away in sorted(range(1, ny), key=lambda d: -min(d, ny - d)):
        send_a(gx, away)
        send_a(twin, away)
    send_a(twin, 0)
    hear_x(2)
    tell_x(3)
    hear_x(3)
    tell_x(4)
    some = slots_a.at[pl.ds(0, 2 * ny - 1)]
    each(first, has, lambda c: c.wait_send())
    each(second, gives, lambda c: c.wait_send())
    pltpu.make_async_copy(some, some, ga_sem.at[1]).wait()
    for c in range(2):
        both = jnp.zeros((1, 128), F32)
        for i in range(ny):
            both = both + jnp.where((core == c) & (gy == i), row, slots_a[c * ny + i])
        row_b[c] = both

    hear_x(4)
    chips = nx // 2
    ring_x = 4 if chips % 4 == 0 else chips
    ring_y = chips // ring_x
    cx0, cy0 = lax.rem(chip, ring_x), chip // ring_x

    def hops(d):
        return min(d[0], ring_x - d[0]) + min(d[1], ring_y - d[1])

    for dx, dy in sorted(
        ((i, j) for i in range(ring_x) for j in range(ring_y) if i + j), key=lambda d: -hops(d)
    ):
        to = lax.rem(cy0 + dy, ring_y) * ring_x + lax.rem(cx0 + dx, ring_x)
        pltpu.make_async_remote_copy(
            row_b, slots_b.at[chip], gb_sem.at[0], gb_sem.at[1],
            device_id=(to * 2 + core, gy), device_id_type=MESH,
        ).start()
    some_b = slots_b.at[pl.ds(0, chips - 1)]
    pltpu.make_async_copy(some, some, ga_sem.at[0]).wait()
    pltpu.make_async_copy(some_b, some_b, gb_sem.at[1]).wait()
    every = jnp.concatenate(
        [
            jnp.where(chip == i, row_b[c], slots_b[i, c])
            for i in range(chips)
            for c in range(2)
        ],
        axis=0,
    )
    lanes = lax.rem(lax.broadcasted_iota(jnp.int32, (nx, 128), 1), 8)

    def over_all(x, i):
        return total(jnp.where(lanes == i, x, 0.0))

    energy = over_all(every, 0)
    step0 = energy / (over_all(every, 1) + EPS)
    next1, next2 = pltpu.roll(every, 127, 1), pltpu.roll(every, 126, 1)
    off = next1 - step0
    renewed = over_all(every + off * off * next2, 2)
    alpha = 1.0 + renewed / (energy + EPS)
    lean = alpha * pltpu.roll(every, 2, 1) - step0
    curved = alpha * alpha * every + lean * (2.0 * alpha * next1 + lean * next2)
    step1 = renewed / (over_all(curved, 5) + EPS)
    c0, c1 = step0 + step1 * alpha, -(step1 * step0)

    x = c0 * coef[0] + c1 * coef[1]
    diag = lax.broadcasted_iota(jnp.int32, (K, 128), 0) == lax.broadcasted_iota(jnp.int32, (K, 128), 1)
    small_ref[0:1] = jnp.sum(jnp.where(diag, x, 0.0), axis=0, keepdims=True)
    small_ref[1:2] = jnp.broadcast_to(c0, (1, 128))
    small_ref[2:3] = jnp.broadcast_to(c1, (1, 128))

    pltpu.make_async_copy(some_b, some_b, gb_sem.at[0]).wait()


def solution(mesh):
    nx, ny = mesh.shape["gx"], mesh.shape["gy"]

    def per_device(basis, mobility, accumulation, residual):
        cells = mobility.shape
        vmem = pltpu.VMEM
        field, small = pl.pallas_call(
            functools.partial(kernel, nx, ny),
            out_shape=(
                vmem((2, *cells), F32),
                vmem((8, 128), F32),
            ),
            in_specs=[pl.BlockSpec(memory_space=pl.ANY)] * 4,
            out_specs=(pl.BlockSpec(memory_space=pltpu.VMEM),) * 2,
            scratch_shapes=[
                vmem(basis.shape, basis.dtype),
                vmem(cells, mobility.dtype),
                vmem(cells, F32),
                vmem(cells, F32),
                pltpu.SemaphoreType.DMA((7,)),
                vmem((2, K, 128), F32),
                vmem((K, 8, 128), F32),
                vmem((K, 2, 8, 128), F32),
                vmem((K, 2, 8, 128), F32),
                vmem((2, 4, 8, 128), F32),
                vmem((2, 4, 8, 128), F32),
                pltpu.SemaphoreType.DMA((2, 4)),
                pltpu.SemaphoreType.DMA((2, 4)),
                vmem((1, 128), F32),
                vmem((2 * ny, 1, 128), F32),
                vmem((2, 1, 128), F32),
                vmem((nx // 2, 2, 1, 128), F32),
                pltpu.SemaphoreType.DMA((2,)),
                pltpu.SemaphoreType.DMA((2,)),
                pltpu.SemaphoreType.REGULAR((5,)),
                pltpu.SemaphoreType.REGULAR((2,)),
                pltpu.SemaphoreType.REGULAR,
            ],
            compiler_params=pltpu.CompilerParams(collective_id=0, has_side_effects=True),
        )(basis, mobility, accumulation, residual)

        def finish(f, s, corr, coarse):
            corr[...] = s[1:2].reshape(1, 1, 128) * f[0] + s[2:3].reshape(1, 1, 128) * f[1]
            coarse[0] = s[0:1, :K]

        return pl.pallas_call(
            finish,
            out_shape=(jax.ShapeDtypeStruct(cells, F32), jax.ShapeDtypeStruct((1, 1, K), F32)),
            in_specs=[pl.BlockSpec(memory_space=pltpu.VMEM)] * 2,
        )(*(pltpu.with_memory_space_constraint(v, pltpu.VMEM) for v in (field, small)))

    cells = P(None, "gy", "gx")
    return jax.shard_map(
        per_device,
        mesh=mesh,
        in_specs=(P(None, None, "gy", "gx"), cells, cells, cells),
        out_specs=(cells, P("gx", "gy", None)),
        check_vma=False,
    )
```

```python
import functools

import jax
import jax.numpy as jnp
from jax import lax
from jax.experimental import pallas as pl
from jax.experimental.pallas import tpu as pltpu
from jax.sharding import PartitionSpec as P


K = 16
EPS = 1e-06
VERTICAL = 0.1
MESH = pl.DeviceIdType.MESH
F32 = jnp.float32


def harmonic(a, b):
    return 2.0 * a * b / (a + b)


def lane_edges(x, lane, side):
    tiles = x.reshape(-1, 8, 128)
    out = jnp.zeros((8, 128), F32)
    for j in range(tiles.shape[0]):
        out = jnp.where(lane == j, tiles[j][:, side : side + 1], out)
    return out


def total(x):
    return jnp.sum(jnp.sum(x, axis=0, keepdims=True), axis=1, keepdims=True)


def signal(sem, x, y):
    pl.semaphore_signal(sem, 1, device_id=(x, y), device_id_type=MESH)


def kernel(
    nx, ny, basis_hbm, mob_hbm, acc_hbm, res_hbm, field, small_ref,
    basis, mob, acc, res, load_sem,
    coef, parts, zx, zy, hsend, ghost, hs_sem, hr_sem,
    row_a, slots_a, row_b, slots_b, ga_sem, gb_sem,
    far_x, far_y, met,
):
    gx, gy = lax.axis_index("gx"), lax.axis_index("gy")
    chip, core = gx // 2, lax.rem(gx, 2)
    twin = gx + 1 - 2 * core
    right, left = lax.rem(gx + 1, nx), lax.rem(gx + nx - 1, nx)
    above, below = lax.rem(gy + 1, ny), lax.rem(gy + ny - 1, ny)

    quarters = [pl.ds(k, K // 4) for k in range(0, K, K // 4)]
    loads = [
        pltpu.make_async_copy(mob_hbm, mob, load_sem.at[0]),
        pltpu.make_async_copy(res_hbm, res, load_sem.at[1]),
        *(
            pltpu.make_async_copy(basis_hbm.at[part], basis.at[part], load_sem.at[2 + i])
            for i, part in enumerate(quarters)
        ),
        pltpu.make_async_copy(acc_hbm, acc, load_sem.at[6]),
    ]
    for c in loads:
        c.start()

    has = [gx < nx - 1, gx > 0, gy < ny - 1, gy > 0]
    barrier = pltpu.get_barrier_semaphore()
    near_y = [d for d in (1, -1, 2, -2) if 2 * abs(d) < ny]
    for d in near_y:
        signal(barrier, gx, lax.rem(gy + ny + d, ny))
    reach_y = [d for d in (2, 4, 8, 16, 32) if d < ny // 2]
    reach_x = [d for d in (1, 2, 4, 8, 16, 32) if d < nx]

    def signal_x(sem, d):
        @pl.when(gx + d < nx)
        def _():
            signal(sem, lax.rem(gx + d, nx), gy)

        @pl.when(gx >= d)
        def _():
            signal(sem, lax.rem(gx + nx - d, nx), gy)

    def count_x(d):
        return jnp.where(gx + d < nx, 1, 0) + jnp.where(gx >= d, 1, 0)

    signal_x(barrier, 1)

    def tell_y(i):
        if i < len(reach_y):
            signal(far_y.at[i], gx, lax.rem(gy + reach_y[i], ny))
            signal(far_y.at[i], gx, lax.rem(gy + ny - reach_y[i], ny))

    def tell_x(i):
        if i < len(reach_x):
            signal_x(far_x.at[i], reach_x[i])

    def hear_y(i):
        if i < len(reach_y):
            pl.semaphore_wait(far_y.at[i], 2)

    def hear_x(i):
        if i < len(reach_x):
            pl.semaphore_wait(far_x.at[i], count_x(reach_x[i]))

    lane = lax.broadcasted_iota(jnp.int32, (8, 128), 1)
    sub = lax.broadcasted_iota(jnp.int32, (8, 128), 0)
    cz, cy, cx = mob.shape

    loads[0].wait()
    m = mob[...].astype(F32)
    m_east, m_west = lane_edges(m, lane, cx - 1), lane_edges(m, lane, 0)
    for z in range(cz):
        hsend[0, 2, cz + z : cz + z + 1] = m[z, cy - 1 : cy]
        hsend[0, 3, cz + z : cz + z + 1] = m[z, 0:1]
    loads[1].wait()
    r = res[...]
    for k in range(K):
        if k % (K // 4) == 0:
            loads[2 + k // (K // 4)].wait()
        parts[k] = jnp.sum((basis[k].astype(F32) * r).reshape(-1, 8, 128), axis=0)
    b = jnp.sum(jnp.sum(parts[...], axis=1), axis=1, keepdims=True)
    coef[0] = jnp.broadcast_to(b, (K, 128))

    def prolong(which):
        p = jnp.zeros((cz, cy, cx), F32)
        for k in range(K):
            p = p + basis[k].astype(F32) * coef[which, k : k + 1].reshape(1, 1, 128)
        return p

    p0 = prolong(0)
    p0_east, p0_west = lane_edges(p0, lane, cx - 1), lane_edges(p0, lane, 0)
    shifted = (lane >= 16) & (lane < 32)
    hsend[0, 0] = jnp.where(shifted, pltpu.roll(m_east, 16, 1), p0_east)
    hsend[0, 1] = jnp.where(shifted, pltpu.roll(m_west, 16, 1), p0_west)
    for z in range(cz):
        hsend[0, 2, z : z + 1] = p0[z, cy - 1 : cy]
        hsend[0, 3, z : z + 1] = p0[z, 0:1]

    pl.semaphore_wait(barrier, count_x(1) + len(near_y))

    def halo(step):
        to = [(right, gy), (left, gy), (gx, above), (gx, below)]
        return [
            pltpu.make_async_remote_copy(
                hsend.at[step, s], ghost.at[step, s ^ 1],
                hs_sem.at[step, s], hr_sem.at[step, s ^ 1],
                device_id=to[s], device_id_type=MESH,
            )
            for s in range(4)
        ]

    middle = ny // 2
    weighs = [has[0], gx < 0, has[2] & (gy < middle), has[3] & (gy > middle)]
    gives = [gx < 0, has[1], has[2] & (gy >= middle), has[3] & (gy <= middle)]

    def arrive(step, sides):
        for s in range(4):

            @pl.when(sides[s])
            def _(s=s):
                here = ghost.at[step, s]
                pltpu.make_async_copy(here, here, hr_sem.at[step, s]).wait()

    def each(copies, sides, act):
        for s in range(4):

            @pl.when(sides[s])
            def _(c=copies[s]):
                act(c)

    first = halo(0)
    each(first, has, lambda c: c.start())
    tell_y(0)
    tell_x(0)

    tx = harmonic(m, pltpu.roll(m, cx - 1, 2))
    lane3 = lax.broadcasted_iota(jnp.int32, (cz, cy, cx), 2)
    row3 = lax.broadcasted_iota(jnp.int32, (cz, cy, cx), 1)
    tx = jnp.where(lane3 == cx - 1, 0.0, tx)
    ty = jnp.where(row3 == cy - 1, 0.0, harmonic(m, pltpu.roll(m, cy - 1, 1)))
    tz = VERTICAL * harmonic(m[:-1], m[1:])
    loads[6].wait()
    ac = acc[...]

    def differences(p):
        return p - pltpu.roll(p, cx - 1, 2), p - pltpu.roll(p, cy - 1, 1), p[:-1] - p[1:]

    d0x, d0y, d0z = differences(p0)
    fx, fy, fz = tx * d0x, ty * d0y, tz * d0z
    jp = ac * p0 + (fx - pltpu.roll(fx, 1, 2)) + (fy - pltpu.roll(fy, 1, 1))
    none = jnp.zeros((1, cy, cx), F32)
    jp = jp + jnp.concatenate([fz, none], axis=0) - jnp.concatenate([none, fz], axis=0)
    for k in range(K):
        zk = basis[k].astype(F32)
        parts[k] = jnp.sum((zk * jp).reshape(-1, 8, 128), axis=0)
        zx[k, 0] = lane_edges(zk, lane, cx - 1)
        zx[k, 1] = lane_edges(zk, lane, 0)
        zero = jnp.zeros((cz, 128), F32)
        zy[k, 0] = jnp.concatenate([zk[z, cy - 1 : cy] for z in range(cz)] + [zero], axis=0)
        zy[k, 1] = jnp.concatenate([zk[z, 0:1] for z in range(cz)] + [zero], axis=0)

    field[0] = p0
    hear_y(0)
    tell_y(1)
    edge_p0 = [p0_east, p0_west, hsend[0, 2], hsend[0, 3]]

    arrive(0, has)
    t_edge, jump, flux = [], [], []
    for s in range(4):
        g = ghost[0, s]
        if s < 2:
            mine, other = (m_east, m_west)[s], pltpu.roll(g, 128 - 16, 1)
            inside = lane < 16
        else:
            mine, other = pltpu.roll(edge_p0[s], 8 - cz, 0), pltpu.roll(g, 8 - cz, 0)
            inside = sub < cz
        joined = inside & has[s]
        t = jnp.where(joined, harmonic(mine, other), 0.0)
        d = jnp.where(joined, edge_p0[s] - g, 0.0)
        t_edge.append((joined, t))
        jump.append(d)
        flux.append(t * d)
    for k in range(K):
        parts[k] = parts[k] + (zx[k, 0] * flux[0] + zx[k, 1] * flux[1]) + (
            zy[k, 0] * flux[2] + zy[k, 1] * flux[3]
        )
    q = jnp.sum(jnp.sum(parts[...], axis=1), axis=1, keepdims=True)
    coef[1] = jnp.broadcast_to(q, (K, 128))

    edge_p1 = [jnp.zeros((8, 128), F32) for _ in range(4)]
    for k in range(K):
        qk = coef[1, k : k + 1]
        edge_p1[0] = edge_p1[0] + zx[k, 0] * qk
        edge_p1[1] = edge_p1[1] + zx[k, 1] * qk
        edge_p1[2] = edge_p1[2] + zy[k, 0] * qk
        edge_p1[3] = edge_p1[3] + zy[k, 1] * qk
    for s in range(4):
        hsend[1, s] = edge_p1[s]
    second = halo(1)
    each(second, gives, lambda c: c.start())
    hear_x(0)
    tell_x(1)

    bv, qv = coef[0], coef[1]
    qq = jnp.sum(qv * qv, axis=0, keepdims=True)
    bq = jnp.sum(bv * qv, axis=0, keepdims=True)
    bb = jnp.sum(bv * bv, axis=0, keepdims=True)
    ratio = jnp.where(qq > 0.0, bq / jnp.where(qq > 0.0, qq, 1.0), 0.0)
    rest = bv - ratio * qv
    rr = jnp.sum(rest * rest, axis=0, keepdims=True)

    p1 = prolong(1)
    field[1] = p1
    d1x, d1y, d1z = differences(p1)
    ratio3 = ratio.reshape(1, 1, 128)
    pr = p0 - ratio3 * p1
    rx, ry, rz = d0x - ratio3 * d1x, d0y - ratio3 * d1y, d0z - ratio3 * d1z

    def inside_energy(a, ax, ay, az, c, cxx, cyy, czz):
        e = ac * a * c + tx * ax * cxx + ty * ay * cyy
        return jnp.sum(e.reshape(-1, 8, 128), axis=0) + jnp.sum(
            (tz * az * czz).reshape(-1, 8, 128), axis=0
        )

    e_rr = inside_energy(pr, rx, ry, rz, pr, rx, ry, rz)
    e_rp = inside_energy(pr, rx, ry, rz, p1, d1x, d1y, d1z)
    e_pp = inside_energy(p1, d1x, d1y, d1z, p1, d1x, d1y, d1z)

    hear_y(1)
    signal(met, twin, gy)
    hear_x(1)
    tell_x(2)
    arrive(1, weighs)
    for s in (0, 2, 3):
        joined, t = t_edge[s]
        mine = joined & weighs[s]
        dp = jnp.where(mine, edge_p1[s] - ghost[1, s], 0.0)
        dr = jump[s] - ratio * dp
        t = jnp.where(mine, t, 0.0)
        e_rr = e_rr + t * dr * dr
        e_rp = e_rp + t * dr * dp
        e_pp = e_pp + t * dp * dp

    lane1 = lax.broadcasted_iota(jnp.int32, (1, 128), 1)
    row = jnp.zeros((1, 128), F32)
    for i, v in enumerate([bb, bq, rr, ratio, qq, total(e_rr), total(e_rp), total(e_pp)]):
        row = jnp.where(lane1 == gy * 8 + i, v, row)
    row_a[...] = row
    pl.semaphore_wait(met, 1)

    def send_a(x, away):
        pltpu.make_async_remote_copy(
            row_a, slots_a.at[core * ny + gy], ga_sem.at[0], ga_sem.at[1],
            device_id=(x, lax.rem(gy + away, ny)), device_id_type=MESH,
        ).start()

    for away in sorted(range(1, ny), key=lambda d: -min(d, ny - d)):
        send_a(gx, away)
        send_a(twin, away)
    send_a(twin, 0)
    hear_x(2)
    tell_x(3)
    hear_x(3)
    tell_x(4)
    some = slots_a.at[pl.ds(0, 2 * ny - 1)]
    each(first, has, lambda c: c.wait_send())
    each(second, gives, lambda c: c.wait_send())
    pltpu.make_async_copy(some, some, ga_sem.at[1]).wait()
    for c in range(2):
        both = jnp.zeros((1, 128), F32)
        for i in range(ny):
            both = both + jnp.where((core == c) & (gy == i), row, slots_a[c * ny + i])
        row_b[c] = both

    hear_x(4)
    chips = nx // 2
    ring_x = 4 if chips % 4 == 0 else chips
    ring_y = chips // ring_x
    cx0, cy0 = lax.rem(chip, ring_x), chip // ring_x

    def hops(d):
        return min(d[0], ring_x - d[0]) + min(d[1], ring_y - d[1]) + (d[0] > 1) + (d[1] > 1)

    for dx, dy in sorted(
        ((i, j) for i in range(ring_x) for j in range(ring_y) if i + j), key=lambda d: -hops(d)
    ):
        to = lax.rem(cy0 + dy, ring_y) * ring_x + lax.rem(cx0 + dx, ring_x)
        pltpu.make_async_remote_copy(
            row_b, slots_b.at[chip], gb_sem.at[0], gb_sem.at[1],
            device_id=(to * 2 + core, gy), device_id_type=MESH,
        ).start()
    some_b = slots_b.at[pl.ds(0, chips - 1)]
    pltpu.make_async_copy(some, some, ga_sem.at[0]).wait()
    pltpu.make_async_copy(some_b, some_b, gb_sem.at[1]).wait()
    every = jnp.concatenate(
        [
            jnp.where(chip == i, row_b[c], slots_b[i, c])
            for i in range(chips)
            for c in range(2)
        ],
        axis=0,
    )
    lanes = lax.rem(lax.broadcasted_iota(jnp.int32, (nx, 128), 1), 8)

    def over_all(x, i):
        return total(jnp.where(lanes == i, x, 0.0))

    energy = over_all(every, 0)
    step0 = energy / (over_all(every, 1) + EPS)
    next1, next2 = pltpu.roll(every, 127, 1), pltpu.roll(every, 126, 1)
    off = next1 - step0
    renewed = over_all(every + off * off * next2, 2)
    alpha = 1.0 + renewed / (energy + EPS)
    lean = alpha * pltpu.roll(every, 2, 1) - step0
    curved = alpha * alpha * every + lean * (2.0 * alpha * next1 + lean * next2)
    step1 = renewed / (over_all(curved, 5) + EPS)
    c0, c1 = step0 + step1 * alpha, -(step1 * step0)

    x = c0 * coef[0] + c1 * coef[1]
    diag = lax.broadcasted_iota(jnp.int32, (K, 128), 0) == lax.broadcasted_iota(jnp.int32, (K, 128), 1)
    small_ref[0:1] = jnp.sum(jnp.where(diag, x, 0.0), axis=0, keepdims=True)
    small_ref[1:2] = jnp.broadcast_to(c0, (1, 128))
    small_ref[2:3] = jnp.broadcast_to(c1, (1, 128))

    pltpu.make_async_copy(some_b, some_b, gb_sem.at[0]).wait()


def solution(mesh):
    nx, ny = mesh.shape["gx"], mesh.shape["gy"]

    def per_device(basis, mobility, accumulation, residual):
        cells = mobility.shape
        vmem = pltpu.VMEM
        field, small = pl.pallas_call(
            functools.partial(kernel, nx, ny),
            out_shape=(
                vmem((2, *cells), F32),
                vmem((8, 128), F32),
            ),
            in_specs=[pl.BlockSpec(memory_space=pl.ANY)] * 4,
            out_specs=(pl.BlockSpec(memory_space=pltpu.VMEM),) * 2,
            scratch_shapes=[
                vmem(basis.shape, basis.dtype),
                vmem(cells, mobility.dtype),
                vmem(cells, F32),
                vmem(cells, F32),
                pltpu.SemaphoreType.DMA((7,)),
                vmem((2, K, 128), F32),
                vmem((K, 8, 128), F32),
                vmem((K, 2, 8, 128), F32),
                vmem((K, 2, 8, 128), F32),
                vmem((2, 4, 8, 128), F32),
                vmem((2, 4, 8, 128), F32),
                pltpu.SemaphoreType.DMA((2, 4)),
                pltpu.SemaphoreType.DMA((2, 4)),
                vmem((1, 128), F32),
                vmem((2 * ny, 1, 128), F32),
                vmem((2, 1, 128), F32),
                vmem((nx // 2, 2, 1, 128), F32),
                pltpu.SemaphoreType.DMA((2,)),
                pltpu.SemaphoreType.DMA((2,)),
                pltpu.SemaphoreType.REGULAR((5,)),
                pltpu.SemaphoreType.REGULAR((2,)),
                pltpu.SemaphoreType.REGULAR,
            ],
            compiler_params=pltpu.CompilerParams(collective_id=0, has_side_effects=True),
        )(basis, mobility, accumulation, residual)

        def finish(f, s, corr, coarse):
            corr[...] = s[1:2].reshape(1, 1, 128) * f[0] + s[2:3].reshape(1, 1, 128) * f[1]
            coarse[0] = s[0:1, :K]

        return pl.pallas_call(
            finish,
            out_shape=(jax.ShapeDtypeStruct(cells, F32), jax.ShapeDtypeStruct((1, 1, K), F32)),
            in_specs=[pl.BlockSpec(memory_space=pltpu.VMEM)] * 2,
        )(*(pltpu.with_memory_space_constraint(v, pltpu.VMEM) for v in (field, small)))

    cells = P(None, "gy", "gx")
    return jax.shard_map(
        per_device,
        mesh=mesh,
        in_specs=(P(None, None, "gy", "gx"), cells, cells, cells),
        out_specs=(cells, P("gx", "gy", None)),
        check_vma=False,
    )
```
